32 devices in a mesh: row: 8 (over z, x), col: 4 (over y, core).
Axes of the slice: x: 2, y: 2, z: 4, core: 2. Of those that a mesh axis runs over, the one named last changes fastest.
Arguments:
- graph_one: bfloat16 [4096, 4096], P('row'), may hold values from -64 to 64
- graph_two: bfloat16 [2048, 2048], P('col'), may hold values from -64 to 64
- coupling: float32 [4096, 2048], P('row', 'col'), may hold values from 0.2 to 5
- sizes_one: int32 [8], replicated, may hold values from 256 to 512
- sizes_two: int32 [4], replicated, may hold values from 256 to 512
Outputs:
- new_coupling: float32 [4096, 2048], P('row', 'col')
- row_potential: float32 [4096], P('row')
- col_potential: float32 [2048], P('col')
The draws below stay inside these ranges and needn't reach their ends.
All inputs are finite; a program needn't handle non-finite values.
Results may differ from the reference program's by a relative error of at most 0.007.
The reference program's roundings to bfloat16 on the way (of `rounded_plan` and `first_product`) count: a program that leaves them out, or rounds other values in their place, can miss the bound.
Values may be sent and summed in bfloat16 or wider, within the bound.
No kernel may reach another device: no remote copies, remote signals or barrier semaphores. Data moves between devices by JAX's collectives and lax.ppermute only.
A program may use at most 128 MiB of HBM per device.

```python
import math
import jax
import jax.numpy as jnp
from jax import lax

BLOCK = 512
SWEEPS = 5
N1 = 4096
N2 = 2048
NB1 = 8
NB2 = 4


def symmetric_draw(key, count):
    raw = jnp.clip(jax.random.normal(jax.random.fold_in(key, 11), (count, count), jnp.float32), -5.0, 5.0)
    matrix = (raw + raw.T) * 0.5 ** 0.5
    return matrix.astype(jnp.bfloat16)


def draw_graph_one(key, part):
    return symmetric_draw(jax.random.fold_in(key, 21), N1)


def draw_graph_two(key, part):
    return symmetric_draw(jax.random.fold_in(key, 22), N2)


def with_ends(drawn, key, smallest, largest):
    extent = drawn.shape
    index_at = [jax.random.randint(jax.random.fold_in(key, axis), (), 0, extent[axis]) for axis in range(len(extent))]
    drawn = drawn.at[tuple(index_at)].set(smallest)
    longest = extent.index(max(extent))
    index_at[longest] = (index_at[longest] + 1) % extent[longest]
    return drawn.at[tuple(index_at)].set(largest)


def shard_levels(stream_key, shape, shards, least, top_value):
    gain = 1.0
    for position, blocks in shards:
        heights = jax.random.uniform(jax.random.fold_in(jax.random.fold_in(stream_key, 6), position), (blocks,), jnp.float32, least / len(shards), top_value / len(shards))
        gain = gain * jnp.repeat(jnp.exp(heights), shape[position] // blocks).reshape((-1,) + (1,) * (len(shape) - 1 - position))
    return gain


def setup_inputs(seed: int = 0) -> dict:
    streams_of = jax.random.split(jax.random.key(seed), 6)
    return {
        "graph_one": draw_graph_one(jax.random.fold_in(streams_of[5], 71), 0),
        "graph_two": draw_graph_two(jax.random.fold_in(streams_of[5], 71), 0),
        "coupling": jnp.clip(jnp.exp(math.log(5.0) - 3.218876 * jax.random.uniform(streams_of[2], (N1, N2), jnp.float32) ** shard_levels(streams_of[2], (N1, N2), ((0, 8), (1, 4)), -0.2, 0.2)), 0.2, 5.0),
        "sizes_one": with_ends(jax.random.randint(streams_of[3], (NB1,), BLOCK // 2, BLOCK + 1), jax.random.fold_in(streams_of[3], 1), BLOCK // 2, BLOCK).astype(jnp.int32),
        "sizes_two": with_ends(jax.random.randint(streams_of[4], (NB2,), BLOCK // 2, BLOCK + 1), jax.random.fold_in(streams_of[4], 1), BLOCK // 2, BLOCK).astype(jnp.int32),
    }


def reference(graph_one, graph_two, coupling, sizes_one, sizes_two):
    count_one = graph_one.shape[0]
    count_two = graph_two.shape[0]
    live_one = (jnp.arange(count_one, dtype=jnp.int32) % BLOCK < jnp.repeat(sizes_one, BLOCK, total_repeat_length=count_one)).astype(jnp.int32)
    live_two = (jnp.arange(count_two, dtype=jnp.int32) % BLOCK < jnp.repeat(sizes_two, BLOCK, total_repeat_length=count_two)).astype(jnp.int32)
    total_one = jnp.sum(sizes_one).astype(jnp.float32)
    total_two = jnp.sum(sizes_two).astype(jnp.float32)
    mask_one = live_one > 0
    mask_two = live_two > 0
    live_both = mask_one[:, None] & mask_two[None, :]
    rounded_plan = jnp.where(live_both, coupling, jnp.float32(0.0)).astype(jnp.bfloat16)
    first_product = jnp.dot(graph_one, rounded_plan, preferred_element_type=jnp.float32).astype(jnp.bfloat16)
    cross_term = jnp.dot(first_product, graph_two, preferred_element_type=jnp.float32)
    row_const = lax.optimization_barrier(jnp.sum(jnp.square(graph_one.astype(jnp.float32)) * live_one.astype(jnp.float32)[None, :], axis=1)) / total_one
    col_const = lax.optimization_barrier(jnp.sum(jnp.square(graph_two.astype(jnp.float32)) * live_two.astype(jnp.float32)[None, :], axis=1)) / total_two
    mass_scale = float(count_one * count_two)
    epsilon = 1.0 / math.sqrt(mass_scale)
    reduced_cost = -2.0 / mass_scale * cross_term
    reduced_col = jnp.zeros((count_two,), jnp.float32)
    reduced_row = jnp.zeros((count_one,), jnp.float32)
    for sweep_index in range(SWEEPS):
        row_values = (reduced_col[None, :] - reduced_cost) / epsilon
        row_lse = jax.nn.logsumexp(jnp.where(mask_two[None, :], row_values, -jnp.inf), axis=1)
        reduced_row = jnp.where(mask_one, -epsilon * jnp.log(total_one) - epsilon * row_lse, jnp.float32(0.0))
        col_values = (reduced_row[:, None] - reduced_cost) / epsilon
        col_lse = jax.nn.logsumexp(jnp.where(mask_one[:, None], col_values, -jnp.inf), axis=0)
        reduced_col = jnp.where(mask_two, -epsilon * jnp.log(total_two) - epsilon * col_lse, jnp.float32(0.0))
    exponent = (reduced_row[:, None] + reduced_col[None, :] - reduced_cost) / epsilon
    new_coupling = jnp.where(live_both, mass_scale * jnp.exp(exponent), jnp.float32(0.0))
    row_potential = jnp.where(mask_one, reduced_row + row_const, jnp.float32(0.0))
    col_potential = jnp.where(mask_two, reduced_col + col_const, jnp.float32(0.0))
    return (new_coupling, row_potential, col_potential)
```

```python
import math

import jax
import jax.numpy as jnp
from jax import lax
from jax.sharding import PartitionSpec as P

BLOCK = 512
SWEEPS = 5


very_low = -1e30


def live_slots(sizes, begin, count):
    mine = lax.dynamic_slice_in_dim(sizes, begin // BLOCK, count // BLOCK)
    slot = lax.broadcasted_iota(jnp.int32, (count // BLOCK, BLOCK), 1)
    return (slot < mine[:, None]).reshape(count)


def merge(parts):
    highest = jnp.max(parts, axis=0)
    return highest + jnp.log(jnp.sum(jnp.exp(parts - highest[None]), axis=0))


def across_columns(values):
    highest = jnp.max(values, axis=1)
    mine = highest + jnp.log(jnp.sum(jnp.exp(values - highest[:, None]), axis=1))
    count = lax.axis_size("col")
    parts = [mine]
    for step in range(1, count):
        parts.append(lax.ppermute(mine, "col", [(i, (i + step) % count) for i in range(count)]))
    return merge(jnp.stack(parts))


def across_rows(values):
    highest = jnp.max(values, axis=0)
    mine = highest + jnp.log(jnp.sum(jnp.exp(values - highest[None, :]), axis=0))
    count = lax.axis_size("row")
    parts = lax.all_to_all(
        jnp.broadcast_to(mine[None, None], (count, 1) + mine.shape), "row", 0, 0, tiled=True
    )
    return merge(parts[:, 0])


def body(graph_one, graph_two, coupling, sizes_one, sizes_two):
    local_rows, count_one = graph_one.shape
    local_cols, count_two = graph_two.shape
    row_begin = lax.axis_index("row") * local_rows
    col_begin = lax.axis_index("col") * local_cols
    live_rows = live_slots(sizes_one, row_begin, local_rows)
    live_cols = live_slots(sizes_two, col_begin, local_cols)
    total_one = jnp.sum(sizes_one).astype(jnp.float32)
    total_two = jnp.sum(sizes_two).astype(jnp.float32)
    live_both = live_rows[:, None] & live_cols[None, :]
    rounded_plan = jnp.where(live_both, coupling, jnp.float32(0.0)).astype(jnp.bfloat16)
    whole_plan = lax.all_gather(rounded_plan, "row", axis=0, tiled=True)
    first_product = jnp.dot(graph_one, whole_plan, preferred_element_type=jnp.float32).astype(
        jnp.bfloat16
    )
    whole_first = lax.all_gather(first_product, "col", axis=1, tiled=True)
    cross_term = lax.dot_general(
        whole_first, graph_two, (((1,), (1,)), ((), ())), preferred_element_type=jnp.float32
    )
    all_one = live_slots(sizes_one, 0, count_one)
    all_two = live_slots(sizes_two, 0, count_two)
    row_const = jnp.sum(
        jnp.where(all_one[None, :], jnp.square(graph_one.astype(jnp.float32)), 0.0), axis=1
    ) / total_one
    col_const = jnp.sum(
        jnp.where(all_two[None, :], jnp.square(graph_two.astype(jnp.float32)), 0.0), axis=1
    ) / total_two
    mass_scale = float(count_one * count_two)
    epsilon = 1.0 / math.sqrt(mass_scale)
    gain = 2.0 / mass_scale / epsilon * cross_term
    scaled_col = jnp.zeros((local_cols,), jnp.float32)
    for sweep_index in range(SWEEPS):
        shown = jnp.where(live_cols, scaled_col, very_low)
        scaled_row = -jnp.log(total_one) - across_columns(shown[None, :] + gain)
        shown = jnp.where(live_rows, scaled_row, very_low)
        scaled_col = -jnp.log(total_two) - across_rows(shown[:, None] + gain)
    exponent = scaled_row[:, None] + scaled_col[None, :] + gain
    new_coupling = jnp.where(live_both, mass_scale * jnp.exp(exponent), jnp.float32(0.0))
    row_potential = jnp.where(live_rows, epsilon * scaled_row + row_const, jnp.float32(0.0))
    col_potential = jnp.where(live_cols, epsilon * scaled_col + col_const, jnp.float32(0.0))
    return (new_coupling, row_potential, col_potential)


def solution(mesh):
    return jax.shard_map(
        body,
        mesh=mesh,
        in_specs=(P("row", None), P("col", None), P("row", "col"), P(), P()),
        out_specs=(P("row", "col"), P("row"), P("col")),
        check_vma=False,
    )
```
